32 devices in a mesh: freq: 2 (over core), vs: 16 (over z, y, x).
Axes of the slice: x: 2, y: 2, z: 4, core: 2. Of those that a mesh axis runs over, the one named last changes fastest.
Arguments:
- kernel: bfloat16 [4, 2, 256, 16384], P('freq', None, None, 'vs'), may hold values from -0.03125 to 0.03125
- sources: bfloat16 [4, 2, 512, 16384], P('freq', None, 'vs'), may hold values from -6 to 6
- observed: float32 [256, 160, 512], P('freq', None, 'vs'), may hold values from -6 to 6
- gate_start: int32 [256], P('freq'), may hold values from 0 to 80, as said below
- gate_length: int32 [256], P('freq'), may hold values from 1 to 160
Outputs:
- gradient: bfloat16 [4, 2, 512, 16384], P('freq', None, 'vs')
- misfit: float32 [256, 160, 512], P('freq', None, 'vs')
The draws below stay inside these ranges and needn't reach their ends.
Inputs may be any that keep to these rules, and one draw needn't show every extreme that they name: gate_start + gate_length <= 160 for every receiver.
All inputs are finite; a program needn't handle non-finite values.
Results may differ from the reference program's by a relative error of at most 0.0057.
Values may be sent and summed in bfloat16 or wider, within the bound.
A program may use at most 128 MiB of HBM per device.

```python
import jax
import jax.numpy as jnp
from jax import lax

NS = 16384
NT = 160
RW = 256
NF = 4
NV = 512


def gate_pair(key):
    base_key = jax.random.fold_in(key, 4242)
    key_start, key_spread, key_reach, key_choose = jax.random.split(base_key, 4)
    row_index = jnp.arange(RW, dtype=jnp.int32)
    opening = jax.random.randint(key_start, (RW,), 0, NT // 2 + 1, dtype=jnp.int32)
    chosen = jax.random.randint(key_choose, (), 0, RW, dtype=jnp.int32)
    second_row = (chosen + RW // 2) % RW
    opening = jnp.where(row_index == chosen, 0, opening)
    opening = jnp.where(row_index == second_row, NT // 2, opening)
    spread = jax.random.randint(key_spread, (RW,), 0, 1 << 20, dtype=jnp.int32)
    finish = opening + 1 + spread % (NT - opening)
    reaches = jax.random.randint(key_reach, (RW,), 0, 4, dtype=jnp.int32) == 0
    finish = jnp.where(reaches | (row_index == chosen), NT, finish)
    return (opening, finish - opening)


def draw_gate_start(key, part):
    return gate_pair(key)[0]


def draw_gate_length(key, part):
    return gate_pair(key)[1]


def block_scale(own_key, extent, cuts, smallest, largest):
    def one(dim, blocks):
        steps = jax.random.uniform(jax.random.fold_in(jax.random.fold_in(own_key, 6), dim), (blocks,), jnp.float32, smallest / len(cuts), largest / len(cuts))
        return jnp.repeat(jnp.exp(steps), extent[dim] // blocks).reshape((-1,) + (1,) * (len(extent) - dim - 1))

    factor_of = one(*cuts[0])
    for cut in cuts[1:]:
        factor_of = factor_of * one(*cut)
    return factor_of


def centred(rng, extent, deviation, limit, cuts=(), held_as=jnp.bfloat16):
    drawn = jax.random.normal(rng, extent, jnp.float32) * deviation
    if len(cuts) > 0:
        drawn = block_scale(rng, extent, cuts, -0.22, 0.18) * drawn
    return jnp.clip(drawn, min=-limit, max=limit).astype(held_as)


def setup_inputs(seed: int = 0) -> dict:
    splits = jax.random.split(jax.random.key(seed), 6)
    kernel = centred(splits[0], (NF, 2, RW, NS), (2 * NS) ** -0.5, 0.03125, ((0, 2), (3, 16)))
    sources = centred(splits[1], (NF, 2, NV, NS), 1.0, 6.0, ((0, 2), (2, 16)))
    observed = centred(splits[2], (RW, NT, NV), 1.0, 6.0, ((0, 2), (2, 16)), jnp.float32)
    gate_start = draw_gate_start(jax.random.fold_in(splits[5], 71), 0)
    gate_length = draw_gate_length(jax.random.fold_in(splits[5], 71), 0)
    return dict(kernel=kernel, sources=sources, observed=observed, gate_start=gate_start, gate_length=gate_length)


def forward_one(pair):
    kern, model = pair
    real_part = jnp.dot(kern[0], model[0].T, preferred_element_type=jnp.float32) - jnp.dot(kern[1], model[1].T, preferred_element_type=jnp.float32)
    imag_part = jnp.dot(kern[0], model[1].T, preferred_element_type=jnp.float32) + jnp.dot(kern[1], model[0].T, preferred_element_type=jnp.float32)
    return jnp.stack([real_part, imag_part], 0).astype(jnp.bfloat16)


def adjoint_one(pair):
    kern, spectrum = pair
    real_part = jnp.dot(spectrum[0].T, kern[0], preferred_element_type=jnp.float32) + jnp.dot(spectrum[1].T, kern[1], preferred_element_type=jnp.float32)
    imag_part = jnp.dot(spectrum[1].T, kern[0], preferred_element_type=jnp.float32) - jnp.dot(spectrum[0].T, kern[1], preferred_element_type=jnp.float32)
    factor = (NS / RW) ** 0.5
    return (factor * jnp.stack([real_part, imag_part], 0)).astype(jnp.bfloat16)


def transform_tables(count, samples):
    sample_index = jnp.arange(samples, dtype=jnp.int32)
    bin_index = samples // 4 + jnp.arange(count, dtype=jnp.int32)
    phase = (sample_index[:, None] * bin_index[None, :]) % samples
    theta = (2.0 * jnp.pi / samples) * phase.astype(jnp.float32)
    return jnp.cos(theta), jnp.sin(theta)


def reference(kernel, sources, observed, gate_start, gate_length):
    field = lax.map(forward_one, (kernel, sources))
    count = field.shape[0]
    samples = observed.shape[1]
    cosine, sine = transform_tables(count, samples)
    scale = count ** -0.5
    values = field.astype(jnp.float32)
    highest = lax.Precision.HIGHEST
    signal = scale * (jnp.einsum("tf,frv->rtv", cosine, values[:, 0], precision=highest) - jnp.einsum("tf,frv->rtv", sine, values[:, 1], precision=highest))
    sample_index = jnp.arange(samples, dtype=jnp.int32)
    inside = (sample_index[None, :] >= gate_start[:, None]) & (sample_index[None, :] < (gate_start + gate_length)[:, None])
    gate_mask = inside.astype(jnp.float32)
    misfit = gate_mask[:, :, None] * (signal - observed)
    back_real = scale * jnp.einsum("tf,rtv->frv", cosine, misfit, precision=highest)
    back_imag = -scale * jnp.einsum("tf,rtv->frv", sine, misfit, precision=highest)
    back_spectrum = jnp.stack([back_real, back_imag], 1).astype(jnp.bfloat16)
    gradient = lax.map(adjoint_one, (kernel, back_spectrum))
    return gradient, misfit
```

```python
import functools

import numpy as np

import jax
import jax.numpy as jnp
from jax import lax
from jax.experimental import pallas as pl
from jax.experimental.pallas import tpu as pltpu
from jax.sharding import PartitionSpec as P

MESH = pl.DeviceIdType.MESH


def transform_tables(count, samples):
    sample_index = np.arange(samples)
    bin_index = samples // 4 + np.arange(count)
    phase = sample_index[None, :] * bin_index[:, None] % samples
    theta = 2.0 * np.pi / samples * phase
    scale = count ** (-0.5)
    return np.stack([scale * np.cos(theta), -scale * np.sin(theta)], 1).astype(np.float32)


def body(n, nf, factor, k_hbm, x_hbm, obs_hbm, table, gate, grad_hbm, mis_hbm,
         kbuf, xbuf, pbuf, rbuf, fbuf, obuf, bsend, brecv, gbuf,
         lsem, xs, xr, ps, pr, bs, br, gs, gr):
    f = lax.axis_index("freq")
    me = lax.axis_index("vs")
    local_f, rw = kbuf.shape[0], kbuf.shape[2]
    span = kbuf.shape[3]
    samples, nv, half = obuf.shape

    k_copy = pltpu.make_async_copy(k_hbm, kbuf, lsem.at[0])
    o_copy = pltpu.make_async_copy(obs_hbm, obuf, lsem.at[1])
    m_copy = pltpu.make_async_copy(obuf, mis_hbm, lsem.at[2])

    def columns(j):
        return pl.ds(pl.multiple_of(j * span, span), span)

    def peer(d):
        return lax.rem(me + d, n)

    def origin(d):
        return lax.rem(me + n - d, n)

    def other(e):
        return lax.rem(f + e, nf)

    def x_send(j):
        return pltpu.make_async_remote_copy(
            x_hbm.at[:, :, :, columns(j)], xbuf.at[me], xs.at[j], xr.at[me],
            device_id=(f, j), device_id_type=MESH)

    def x_recv(j):
        return pltpu.make_async_remote_copy(
            x_hbm.at[:, :, :, columns(j)], xbuf.at[j], xs.at[j], xr.at[j],
            device_id=(f, j), device_id_type=MESH)

    def p_send(j, h):
        return pltpu.make_async_remote_copy(
            pbuf.at[j, h], rbuf.at[me, f], ps.at[j, h], pr.at[me, f],
            device_id=(h, j), device_id_type=MESH)

    def p_recv(j, h):
        return pltpu.make_async_remote_copy(
            pbuf.at[j, h], rbuf.at[j, h], ps.at[j, h], pr.at[j, h],
            device_id=(h, j), device_id_type=MESH)

    def b_send(j, h):
        return pltpu.make_async_remote_copy(
            bsend.at[h], brecv.at[me, f], bs.at[j, h], br.at[me, f],
            device_id=(h, j), device_id_type=MESH)

    def b_recv(j, h):
        return pltpu.make_async_remote_copy(
            bsend.at[h], brecv.at[j, h], bs.at[j, h], br.at[j, h],
            device_id=(h, j), device_id_type=MESH)

    def g_send(j):
        return pltpu.make_async_remote_copy(
            gbuf.at[j], grad_hbm.at[:, :, :, columns(me)], gs.at[j], gr.at[me],
            device_id=(f, j), device_id_type=MESH)

    def g_recv(j):
        return pltpu.make_async_remote_copy(
            gbuf.at[j], grad_hbm.at[:, :, :, columns(j)], gs.at[j], gr.at[j],
            device_id=(f, j), device_id_type=MESH)

    x_own = pltpu.make_async_copy(x_hbm.at[:, :, :, columns(me)], xbuf.at[me], xr.at[me])
    p_own = pltpu.make_async_copy(pbuf.at[me, f], rbuf.at[me, f], pr.at[me, f])
    b_own = pltpu.make_async_copy(bsend.at[f], brecv.at[me, f], br.at[me, f])
    g_own = pltpu.make_async_copy(gbuf.at[me], grad_hbm.at[:, :, :, columns(me)], gr.at[me])

    barrier = pltpu.get_barrier_semaphore()
    for e in range(1, nf):
        pl.semaphore_signal(barrier, inc=1, device_id=(other(e), me), device_id_type=MESH)

    @pl.loop(1, n)
    def _(d):
        for e in range(nf):
            pl.semaphore_signal(barrier, inc=1, device_id=(other(e), peer(d)), device_id_type=MESH)

    k_copy.start()
    x_own.start()
    o_copy.start()
    pl.semaphore_wait(barrier, n * nf - 1)

    @pl.loop(1, n)
    def _(d):
        x_send(peer(d)).start()

    k_copy.wait()

    def forward(j):
        for i in range(local_f):
            xr_, xi_ = xbuf[j, i, 0], xbuf[j, i, 1]
            kr_, ki_ = kbuf[i, 0], kbuf[i, 1]
            x2 = jnp.concatenate([xr_, xi_], 0)
            dims = (((1,), (1,)), ((), ()))
            pr_ = lax.dot_general(x2, kr_, dims, preferred_element_type=jnp.float32)
            pi_ = lax.dot_general(x2, ki_, dims, preferred_element_type=jnp.float32)
            real = (pr_[:nv] - pi_[nv:]).astype(jnp.bfloat16)
            imag = (pr_[nv:] + pi_[:nv]).astype(jnp.bfloat16)
            for h in range(nf):
                pbuf[j, h, i, 0] = real[:, h * half:(h + 1) * half]
                pbuf[j, h, i, 1] = imag[:, h * half:(h + 1) * half]

    x_own.wait()
    forward(me)
    p_own.start()
    for e in range(1, nf):
        p_send(me, other(e)).start()

    @pl.loop(1, n)
    def _(d):
        j = origin(d)
        x_recv(j).wait_recv()
        forward(j)
        for e in range(nf):
            p_send(j, other(e)).start()

    p_own.wait()
    for e in range(1, nf):
        p_recv(me, other(e)).wait_recv()

    @pl.loop(1, n)
    def _(d):
        for e in range(nf):
            p_recv(origin(d), other(e)).wait_recv()

    for h in range(nf):
        for i in range(local_f):
            for c in range(2):
                def add(q, total):
                    return total + rbuf[q, h, i, c].astype(jnp.float32)
                total = lax.fori_loop(0, n, add, jnp.zeros((nv, half), jnp.float32))
                fbuf[h * local_f + i, c] = total.astype(jnp.bfloat16).astype(jnp.float32)

    o_copy.wait()
    count = nf * local_f
    opens = gate[0:1, :]
    closes = gate[1:2, :]
    rows = 16
    for part in range(nv // rows):
        sl = slice(part * rows, (part + 1) * rows)
        fields = [fbuf[q, c, sl] for q in range(count) for c in range(2)]

        def sample(t, totals):
            weights = [table[q * samples + t] for q in range(2 * count)]
            signal = fields[0] * weights[0]
            for q in range(1, 2 * count):
                signal = signal + fields[q] * weights[q]
            inside = (opens <= t) & (t < closes)
            misfit = jnp.where(inside, signal - obuf[t, sl], 0.0)
            obuf[t, sl] = misfit
            return tuple(totals[q] + misfit * weights[q] for q in range(2 * count))

        zero = jnp.zeros((rows, half), jnp.float32)
        totals = lax.fori_loop(0, samples, sample, (zero,) * (2 * count))
        for q in range(count):
            for c in range(2):
                bsend[q // local_f, q % local_f, c, sl] = totals[2 * q + c].astype(jnp.bfloat16)

    b_own.start()
    for e in range(1, nf):
        b_send(me, other(e)).start()

    @pl.loop(1, n)
    def _(d):
        for e in range(nf):
            b_send(peer(d), other(e)).start()

    m_copy.start()

    def backward(j):
        for i in range(local_f):
            b_r = jnp.concatenate([brecv[j, h, i, 0] for h in range(nf)], 1)
            b_i = jnp.concatenate([brecv[j, h, i, 1] for h in range(nf)], 1)
            left = jnp.concatenate([b_r, b_i], 0)
            right = jnp.concatenate([b_i, -b_r], 0)
            out = jnp.dot(left, kbuf[i, 0], preferred_element_type=jnp.float32)
            out = out + jnp.dot(right, kbuf[i, 1], preferred_element_type=jnp.float32)
            out = (factor * out).astype(jnp.bfloat16)
            gbuf[j, i, 0] = out[:nv]
            gbuf[j, i, 1] = out[nv:]

    b_own.wait()
    for e in range(1, nf):
        b_recv(me, other(e)).wait_recv()
    backward(me)
    g_own.start()

    @pl.loop(1, n)
    def _(d):
        j = origin(d)
        for e in range(nf):
            b_recv(j, other(e)).wait_recv()
        backward(j)
        g_send(j).start()

    for e in range(1, nf):
        p_send(me, other(e)).wait_send()
        b_send(me, other(e)).wait_send()

    @pl.loop(1, n)
    def _(d):
        j = origin(d)
        x_send(j).wait_send()
        for e in range(nf):
            p_send(j, other(e)).wait_send()
            b_send(j, other(e)).wait_send()
        g_send(j).wait_send()
        g_recv(j).wait_recv()

    g_own.wait()
    m_copy.wait()


def local(n, nf, kernel, sources, observed, gate_start, gate_length):
    local_f, _, rw, span = kernel.shape
    nv, ns = sources.shape[2:]
    half, samples = observed.shape[:2]
    count = nf * local_f
    table = jnp.asarray(transform_tables(count, samples).reshape(-1))
    gate = jnp.stack([gate_start, gate_start + gate_length])
    piece = (local_f, 2, nv, half)
    any_spec = pl.BlockSpec(memory_space=pl.ANY)
    dma = pltpu.SemaphoreType.DMA
    gradient, misfit = pl.pallas_call(
        functools.partial(body, n, nf, (ns / rw) ** 0.5),
        out_shape=(
            jax.ShapeDtypeStruct(sources.shape, jnp.bfloat16),
            jax.ShapeDtypeStruct((samples, nv, half), jnp.float32),
        ),
        in_specs=[any_spec, any_spec, any_spec,
                  pl.BlockSpec(memory_space=pltpu.SMEM),
                  pl.BlockSpec(memory_space=pltpu.VMEM)],
        out_specs=(any_spec, any_spec),
        scratch_shapes=[
            pltpu.VMEM(kernel.shape, jnp.bfloat16),
            pltpu.VMEM((n, local_f, 2, nv, span), jnp.bfloat16),
            pltpu.VMEM((n, nf) + piece, jnp.bfloat16),
            pltpu.VMEM((n, nf) + piece, jnp.bfloat16),
            pltpu.VMEM((count, 2, nv, half), jnp.float32),
            pltpu.VMEM((samples, nv, half), jnp.float32),
            pltpu.VMEM((nf,) + piece, jnp.bfloat16),
            pltpu.VMEM((n, nf) + piece, jnp.bfloat16),
            pltpu.VMEM((n, local_f, 2, nv, span), jnp.bfloat16),
            dma((3,)), dma((n,)), dma((n,)),
            dma((n, nf)), dma((n, nf)), dma((n, nf)), dma((n, nf)),
            dma((n,)), dma((n,)),
        ],
        compiler_params=pltpu.CompilerParams(
            collective_id=0, has_side_effects=True, vmem_limit_bytes=40 << 20),
    )(kernel, sources, observed.transpose(1, 2, 0), table, gate)
    return gradient, misfit.transpose(2, 0, 1)


def solution(mesh):
    n, nf = mesh.shape["vs"], mesh.shape["freq"]
    return jax.shard_map(
        functools.partial(local, n, nf),
        mesh=mesh,
        in_specs=(
            P("freq", None, None, "vs"),
            P("freq", None, "vs", None),
            P("freq", None, "vs"),
            P("freq"),
            P("freq"),
        ),
        out_specs=(P("freq", None, "vs", None), P("freq", None, "vs")),
        check_vma=False,
    )
```

```python
import functools

import numpy as np

import jax
import jax.numpy as jnp
from jax import lax
from jax.experimental import pallas as pl
from jax.experimental.pallas import tpu as pltpu
from jax.sharding import PartitionSpec as P

MESH = pl.DeviceIdType.MESH


def transform_tables(count, samples):
    sample_index = np.arange(samples)
    bin_index = samples // 4 + np.arange(count)
    phase = sample_index[None, :] * bin_index[:, None] % samples
    theta = 2.0 * np.pi / samples * phase
    scale = count ** (-0.5)
    return np.stack([scale * np.cos(theta), -scale * np.sin(theta)], 1).astype(np.float32)


def body(n, nf, factor, k_hbm, x_hbm, obs_hbm, table, gate, grad_hbm, mis,
         kbuf, xbuf, acc, pbuf, rbuf, fbuf, obuf, bsend, brecv, gbuf,
         lsem, ks, kr, xs, xr, ps, pr, bs, br, gs, gr):
    f = lax.axis_index("freq")
    me = lax.axis_index("vs")
    m = n // 2
    q = lax.rem(me, m)
    base = me - q
    partner = lax.rem(me + m, n)
    local_f, rw, span = kbuf.shape[1], kbuf.shape[3], kbuf.shape[4]
    samples, nv, half = obuf.shape

    k_copy = pltpu.make_async_copy(k_hbm, kbuf.at[0], lsem.at[0])
    o_copy = pltpu.make_async_copy(obs_hbm, obuf, lsem.at[1])

    def columns(j, b):
        block = lax.rem(j + b * m, n)
        return pl.ds(pl.multiple_of(block * span, span), span)

    def peer(d):
        return lax.rem(q + d, m)

    def origin(d):
        return lax.rem(q + m - d, m)

    def other(e):
        return lax.rem(f + e, nf)

    def receivers(h):
        return pl.ds(pl.multiple_of(h * half, half), half)

    def k_move(i, c):
        return pltpu.make_async_remote_copy(
            k_hbm.at[i, c], kbuf.at[1, i, c], ks.at[i, c], kr.at[i, c],
            device_id=(f, partner), device_id_type=MESH)

    def x_move(t, b, slot):
        return pltpu.make_async_remote_copy(
            x_hbm.at[:, :, :, columns(base + t, b)], xbuf.at[b, :, slot],
            xs.at[t, b], xr.at[slot, b],
            device_id=(f, base + t), device_id_type=MESH)

    def p_move(t, h, i, slot, lane):
        return pltpu.make_async_remote_copy(
            pbuf.at[t, h, i], rbuf.at[slot, lane, i], ps.at[t, h, i], pr.at[slot, lane, i],
            device_id=(h, base + t), device_id_type=MESH)

    def b_move(t, h, slot, lane):
        return pltpu.make_async_remote_copy(
            bsend.at[h], brecv.at[:, slot, :, :, receivers(lane)],
            bs.at[t, h], br.at[slot, lane],
            device_id=(h, base + t), device_id_type=MESH)

    def g_move(t, b, slot):
        return pltpu.make_async_remote_copy(
            gbuf.at[b, t], grad_hbm.at[:, :, :, columns(base + slot, b)],
            gs.at[t, b], gr.at[slot, b],
            device_id=(f, base + t), device_id_type=MESH)

    x_own = [pltpu.make_async_copy(
        x_hbm.at[:, :, :, columns(me, b)], xbuf.at[b, :, q], xr.at[q, b]) for b in range(2)]
    p_own = [pltpu.make_async_copy(
        pbuf.at[q, f, i], rbuf.at[q, f, i], pr.at[q, f, i]) for i in range(local_f)]
    b_own = pltpu.make_async_copy(
        bsend.at[f], brecv.at[:, q, :, :, receivers(f)], br.at[q, f])
    g_own = [pltpu.make_async_copy(
        gbuf.at[b, q], grad_hbm.at[:, :, :, columns(me, b)], gr.at[q, b]) for b in range(2)]

    barrier = pltpu.get_barrier_semaphore()
    pl.semaphore_signal(barrier, inc=1, device_id=(f, partner), device_id_type=MESH)
    for e in range(1, nf):
        pl.semaphore_signal(barrier, inc=1, device_id=(other(e), me), device_id_type=MESH)

    @pl.loop(1, m)
    def _(d):
        for e in range(nf):
            pl.semaphore_signal(
                barrier, inc=1, device_id=(other(e), base + peer(d)), device_id_type=MESH)

    k_copy.start()
    x_own[0].start()
    x_own[1].start()
    o_copy.start()
    pl.semaphore_wait(barrier, m * nf)

    pieces = [(i, c) for i in range(local_f) for c in range(2)]
    for step, (i, c) in enumerate(pieces):
        k_move(i, c).start()
        low = 1 + (m - 1) * step // len(pieces)
        high = 1 + (m - 1) * (step + 1) // len(pieces)

        @pl.loop(low, high)
        def _(d):
            for b in range(2):
                x_move(peer(d), b, q).start()

    k_copy.wait()
    for b in range(2):
        x_own[b].wait()

        @pl.loop(1, m)
        def _(d):
            x_move(origin(d), b, origin(d)).wait_recv()

    def product(b, i, c):
        rows = xbuf[b, i].reshape(m * 2 * nv, span)
        out = lax.dot_general(rows, kbuf[b, i, c], (((1,), (1,)), ((), ())),
                              preferred_element_type=jnp.float32)
        return out.reshape(m, 2, nv, rw)

    for i, c in pieces:
        acc[i, c] = product(0, i, c)

    for i in range(local_f):
        for c in range(2):
            k_move(i, c).wait_recv()
            acc[i, c] += product(1, i, c)

        @pl.loop(0, m)
        def _(t):
            real = (acc[i, 0, t, 0] - acc[i, 1, t, 1]).astype(jnp.bfloat16)
            imag = (acc[i, 0, t, 1] + acc[i, 1, t, 0]).astype(jnp.bfloat16)
            for h in range(nf):
                pbuf[t, h, i, 0] = real[:, h * half:(h + 1) * half]
                pbuf[t, h, i, 1] = imag[:, h * half:(h + 1) * half]

        @pl.loop(1, m)
        def _(d):
            for e in range(nf):
                p_move(peer(d), other(e), i, q, f).start()

        for e in range(1, nf):
            p_move(q, other(e), i, q, f).start()
        p_own[i].start()

    for i in range(local_f):
        p_own[i].wait()
        for e in range(1, nf):
            p_move(q, other(e), i, q, other(e)).wait_recv()

        @pl.loop(1, m)
        def _(d):
            for e in range(nf):
                p_move(origin(d), other(e), i, origin(d), other(e)).wait_recv()

    for h in range(nf):
        for i in range(local_f):
            for c in range(2):
                def add(t, total):
                    return total + rbuf[t, h, i, c].astype(jnp.float32)
                total = lax.fori_loop(0, m, add, jnp.zeros((nv, half), jnp.float32))
                fbuf[h * local_f + i, c] = total.astype(jnp.bfloat16).astype(jnp.float32)

    o_copy.wait()
    count = nf * local_f
    opens = gate[0:1, :]
    closes = gate[1:2, :]
    rows = 16
    for part in range(nv // rows):
        sl = slice(part * rows, (part + 1) * rows)
        fields = [fbuf[k, c, sl] for k in range(count) for c in range(2)]

        def sample(t, totals):
            weights = [table[k * samples + t] for k in range(2 * count)]
            signal = fields[0] * weights[0]
            for k in range(1, 2 * count):
                signal = signal + fields[k] * weights[k]
            inside = (opens <= t) & (t < closes)
            misfit = jnp.where(inside, signal - obuf[t, sl], 0.0)
            mis[t, sl] = misfit
            return tuple(totals[k] + misfit * weights[k] for k in range(2 * count))

        zero = jnp.zeros((rows, half), jnp.float32)
        totals = lax.fori_loop(0, samples, sample, (zero,) * (2 * count))
        for k in range(count):
            for c in range(2):
                bsend[k // local_f, k % local_f, c, sl] = totals[2 * k + c].astype(jnp.bfloat16)

    @pl.loop(1, m)
    def _(d):
        for e in range(nf):
            b_move(peer(d), other(e), q, f).start()

    b_own.start()
    for e in range(1, nf):
        b_move(q, other(e), q, f).start()

    def backward(t):
        for b in range(2):
            for i in range(local_f):
                left = brecv[i, t].reshape(2 * nv, rw)
                one = jnp.dot(left, kbuf[b, i, 0], preferred_element_type=jnp.float32)
                two = jnp.dot(left, kbuf[b, i, 1], preferred_element_type=jnp.float32)
                real = factor * (one[:nv] + two[nv:])
                imag = factor * (one[nv:] - two[:nv])
                gbuf[b, t, i, 0] = real.astype(jnp.bfloat16)
                gbuf[b, t, i, 1] = imag.astype(jnp.bfloat16)

    @pl.loop(1, m)
    def _(d):
        t = origin(d)
        for e in range(nf):
            b_move(t, other(e), t, other(e)).wait_recv()
        backward(t)
        for b in range(2):
            g_move(t, b, q).start()

    b_own.wait()
    for e in range(1, nf):
        b_move(q, other(e), q, other(e)).wait_recv()
    backward(q)
    for b in range(2):
        g_own[b].start()

    for i, c in pieces:
        k_move(i, c).wait_send()
    for e in range(1, nf):
        for i in range(local_f):
            p_move(q, other(e), i, q, f).wait_send()
        b_move(q, other(e), q, f).wait_send()

    @pl.loop(1, m)
    def _(d):
        t = origin(d)
        for e in range(nf):
            for i in range(local_f):
                p_move(t, other(e), i, q, f).wait_send()
            b_move(t, other(e), q, f).wait_send()
        for b in range(2):
            x_move(t, b, q).wait_send()
            g_move(t, b, q).wait_send()
            g_move(t, b, t).wait_recv()

    for b in range(2):
        g_own[b].wait()


def local(n, nf, kernel, sources, observed, gate_start, gate_length):
    local_f, _, rw, span = kernel.shape
    nv, ns = sources.shape[2:]
    half, samples = observed.shape[:2]
    count = nf * local_f
    m = n // 2
    table = jnp.asarray(transform_tables(count, samples).reshape(-1))
    gate = jnp.stack([gate_start, gate_start + gate_length])
    piece = (local_f, 2, nv, half)
    any_spec = pl.BlockSpec(memory_space=pl.ANY)
    hbm_spec = pl.BlockSpec(memory_space=pltpu.HBM)
    vmem_spec = pl.BlockSpec(memory_space=pltpu.VMEM)
    dma = pltpu.SemaphoreType.DMA
    gradient, misfit = pl.pallas_call(
        functools.partial(body, n, nf, (ns / rw) ** 0.5),
        out_shape=(
            jax.ShapeDtypeStruct(sources.shape, jnp.bfloat16),
            jax.ShapeDtypeStruct((samples, nv, half), jnp.float32),
        ),
        in_specs=[hbm_spec, hbm_spec, hbm_spec,
                  pl.BlockSpec(memory_space=pltpu.SMEM), vmem_spec],
        out_specs=(any_spec, vmem_spec),
        scratch_shapes=[
            pltpu.VMEM((2,) + kernel.shape, jnp.bfloat16),
            pltpu.VMEM((2, local_f, m, 2, nv, span), jnp.bfloat16),
            pltpu.VMEM((local_f, 2, m, 2, nv, rw), jnp.float32),
            pltpu.VMEM((m, nf) + piece, jnp.bfloat16),
            pltpu.VMEM((m, nf) + piece, jnp.bfloat16),
            pltpu.VMEM((count, 2, nv, half), jnp.float32),
            pltpu.VMEM((samples, nv, half), jnp.float32),
            pltpu.VMEM((nf,) + piece, jnp.bfloat16),
            pltpu.VMEM((local_f, m, 2, nv, nf * half), jnp.bfloat16),
            pltpu.VMEM((2, m, local_f, 2, nv, span), jnp.bfloat16),
            dma((2,)), dma((local_f, 2)), dma((local_f, 2)),
            dma((m, 2)), dma((m, 2)),
            dma((m, nf, local_f)), dma((m, nf, local_f)),
            dma((m, nf)), dma((m, nf)),
            dma((m, 2)), dma((m, 2)),
        ],
        compiler_params=pltpu.CompilerParams(
            collective_id=0, has_side_effects=True, vmem_limit_bytes=44 << 20),
    )(kernel, sources, observed.transpose(1, 2, 0), table, gate)
    return gradient, misfit.transpose(2, 0, 1)


def solution(mesh):
    n, nf = mesh.shape["vs"], mesh.shape["freq"]
    return jax.shard_map(
        functools.partial(local, n, nf),
        mesh=mesh,
        in_specs=(
            P("freq", None, None, "vs"),
            P("freq", None, "vs", None),
            P("freq", None, "vs"),
            P("freq"),
            P("freq"),
        ),
        out_specs=(P("freq", None, "vs", None), P("freq", None, "vs")),
        check_vma=False,
    )
```

```python
import functools

import numpy as np

import jax
import jax.numpy as jnp
from jax import lax
from jax.experimental import pallas as pl
from jax.experimental.pallas import tpu as pltpu
from jax.sharding import PartitionSpec as P

MESH = pl.DeviceIdType.MESH


def transform_tables(count, samples):
    sample_index = np.arange(samples)
    bin_index = samples // 4 + np.arange(count)
    phase = sample_index[None, :] * bin_index[:, None] % samples
    theta = 2.0 * np.pi / samples * phase
    scale = count ** (-0.5)
    return np.stack([scale * np.cos(theta), -scale * np.sin(theta)], 1).astype(np.float32)


def body(n, nf, factor, k_hbm, x_hbm, obs_hbm, table_hbm, start_hbm, length_hbm, grad_hbm, mis,
         kbuf, xbuf, acc, pbuf, rbuf, fbuf, obuf, bsend, brecv, gbuf,
         table, gate, lsem, ks, kr, xs, xr, ps, pr, bs, br, gs, gr):
    f = lax.axis_index("freq")
    me = lax.axis_index("vs")
    m = n // 2
    q = lax.rem(me, m)
    base = me - q
    partner = lax.rem(me + m, n)
    local_f, rw, span = kbuf.shape[1], kbuf.shape[3], kbuf.shape[4]
    samples, nv, half = obuf.shape

    k_copy = pltpu.make_async_copy(k_hbm, kbuf.at[0], lsem.at[0])
    o_copy = pltpu.make_async_copy(obs_hbm, obuf, lsem.at[1])
    small = [
        pltpu.make_async_copy(table_hbm, table, lsem.at[2]),
        pltpu.make_async_copy(start_hbm, gate.at[0], lsem.at[3]),
        pltpu.make_async_copy(length_hbm, gate.at[1], lsem.at[4]),
    ]

    def columns(j, b):
        block = lax.rem(j + b * m, n)
        return pl.ds(pl.multiple_of(block * span, span), span)

    def peer(s):
        s = jnp.int32(s) - 1
        odd = lax.rem(s, 2)
        low = lax.div(s, 2)
        d = odd * (low + 1) + (1 - odd) * (m - 1 - low)
        if m & (m - 1):
            return lax.rem(q + d, m)
        t = jnp.int32(0)
        bit = 1
        while bit < m:
            t = t + bit * lax.rem(lax.div(q, bit) + lax.div(d, bit), 2)
            bit *= 2
        return t

    def origin(s):
        if m & (m - 1):
            return lax.rem(2 * q + m - peer(s), m)
        return peer(s)

    def other(e):
        return lax.rem(f + e, nf)

    def receivers(h):
        return pl.ds(pl.multiple_of(h * half, half), half)

    def k_move(i, c):
        g, c = c // 2, c % 2
        rows = pl.ds(g * (rw // 2), rw // 2)
        return pltpu.make_async_remote_copy(
            k_hbm.at[i, c, rows], kbuf.at[1, i, c, rows], ks.at[i, c, g], kr.at[i, c, g],
            device_id=(f, partner), device_id_type=MESH)

    def x_move(t, b, slot):
        return pltpu.make_async_remote_copy(
            x_hbm.at[:, :, :, columns(base + t, b)], xbuf.at[b, :, slot],
            xs.at[t, b], xr.at[slot, b],
            device_id=(f, base + t), device_id_type=MESH)

    def p_move(t, h, i, slot, lane):
        return pltpu.make_async_remote_copy(
            pbuf.at[t, h, i], rbuf.at[slot, lane, i], ps.at[t, h, i], pr.at[slot, lane, i],
            device_id=(h, base + t), device_id_type=MESH)

    def b_move(t, h, slot, lane):
        return pltpu.make_async_remote_copy(
            bsend.at[h], brecv.at[:, slot, :, :, receivers(lane)],
            bs.at[t, h], br.at[slot, lane],
            device_id=(h, base + t), device_id_type=MESH)

    def g_move(t, b, slot):
        return pltpu.make_async_remote_copy(
            gbuf.at[b, t], grad_hbm.at[:, :, :, columns(base + slot, b)],
            gs.at[t, b], gr.at[slot, b],
            device_id=(f, base + t), device_id_type=MESH)

    x_own = [pltpu.make_async_copy(
        x_hbm.at[:, :, :, columns(me, b)], xbuf.at[b, :, q], xr.at[q, b]) for b in range(2)]
    p_own = [pltpu.make_async_copy(
        pbuf.at[q, f, i], rbuf.at[q, f, i], pr.at[q, f, i]) for i in range(local_f)]
    b_own = pltpu.make_async_copy(
        bsend.at[f], brecv.at[:, q, :, :, receivers(f)], br.at[q, f])
    g_own = [pltpu.make_async_copy(
        gbuf.at[b, q], grad_hbm.at[:, :, :, columns(me, b)], gr.at[q, b]) for b in range(2)]

    barrier = pltpu.get_barrier_semaphore()
    pl.semaphore_signal(barrier, inc=1, device_id=(f, partner), device_id_type=MESH)
    for e in range(1, nf):
        pl.semaphore_signal(barrier, inc=1, device_id=(other(e), me), device_id_type=MESH)

    @pl.loop(1, m)
    def _(d):
        for e in range(nf):
            pl.semaphore_signal(
                barrier, inc=1, device_id=(other(e), base + peer(d)), device_id_type=MESH)

    k_copy.start()
    x_own[0].start()
    x_own[1].start()
    o_copy.start()
    for copy in small:
        copy.start()
    pl.semaphore_wait(barrier, m * nf)

    pieces = [(i, c) for i in range(local_f) for c in range(4)]
    k_move(*pieces[0]).start()
    k_move(*pieces[1]).start()
    for step, (i, c) in enumerate(pieces):
        if step >= 2:
            k_move(i, c).start()
        low = 1 + (m - 1) * step // len(pieces)
        high = 1 + (m - 1) * (step + 1) // len(pieces)

        @pl.loop(low, high)
        def _(d):
            for b in range(2):
                x_move(peer(d), b, q).start()

    k_copy.wait()
    for b in range(2):
        x_own[b].wait()

        @pl.loop(1, m)
        def _(d):
            x_move(origin(d), b, origin(d)).wait_recv()

    def product(b, i, c):
        rows = xbuf[b, i].reshape(m * 2 * nv, span)
        out = lax.dot_general(rows, kbuf[b, i, c], (((1,), (1,)), ((), ())),
                              preferred_element_type=jnp.float32)
        return out.reshape(m, 2, nv, rw)

    for i in range(local_f):
        for c in range(2):
            acc[i, c] = product(0, i, c)

    for i in range(local_f):
        for c in range(2):
            k_move(i, c).wait_recv()
            k_move(i, c + 2).wait_recv()
            acc[i, c] += product(1, i, c)

        @pl.loop(0, m)
        def _(t):
            real = (acc[i, 0, t, 0] - acc[i, 1, t, 1]).astype(jnp.bfloat16)
            imag = (acc[i, 0, t, 1] + acc[i, 1, t, 0]).astype(jnp.bfloat16)
            for h in range(nf):
                pbuf[t, h, i, 0] = real[:, h * half:(h + 1) * half]
                pbuf[t, h, i, 1] = imag[:, h * half:(h + 1) * half]

        @pl.loop(1, m)
        def _(d):
            for e in range(nf):
                p_move(peer(d), other(e), i, q, f).start()

        for e in range(1, nf):
            p_move(q, other(e), i, q, f).start()
        p_own[i].start()

    for i in range(local_f):
        p_own[i].wait()
        for e in range(1, nf):
            p_move(q, other(e), i, q, other(e)).wait_recv()

        @pl.loop(1, m)
        def _(d):
            for e in range(nf):
                p_move(origin(d), other(e), i, origin(d), other(e)).wait_recv()

    for h in range(nf):
        for i in range(local_f):
            for c in range(2):
                def add(t, total):
                    return total + rbuf[t, h, i, c].astype(jnp.float32)
                total = lax.fori_loop(0, m, add, jnp.zeros((nv, half), jnp.float32))
                fbuf[h * local_f + i, c] = total.astype(jnp.bfloat16).astype(jnp.float32)

    o_copy.wait()
    for copy in small:
        copy.wait()
    count = nf * local_f
    opens = gate[0]
    closes = opens + gate[1]
    rows = 16
    for part in range(nv // rows):
        sl = slice(part * rows, (part + 1) * rows)
        fields = [fbuf[k, c, sl] for k in range(count) for c in range(2)]

        def sample(t, totals):
            weights = [table[k * samples + t] for k in range(2 * count)]
            signal = fields[0] * weights[0]
            for k in range(1, 2 * count):
                signal = signal + fields[k] * weights[k]
            inside = (opens <= t) & (t < closes)
            misfit = jnp.where(inside, signal - obuf[t, sl], 0.0)
            mis[t, sl] = misfit
            return tuple(totals[k] + misfit * weights[k] for k in range(2 * count))

        zero = jnp.zeros((rows, half), jnp.float32)
        totals = lax.fori_loop(0, samples, sample, (zero,) * (2 * count), unroll=4)
        for k in range(count):
            for c in range(2):
                bsend[k // local_f, k % local_f, c, sl] = totals[2 * k + c].astype(jnp.bfloat16)

    @pl.loop(1, m)
    def _(d):
        for e in range(nf):
            b_move(peer(d), other(e), q, f).start()

    b_own.start()
    for e in range(1, nf):
        b_move(q, other(e), q, f).start()

    def backward(t):
        for b in range(2):
            for i in range(local_f):
                left = brecv[i, t].reshape(2 * nv, rw)
                one = jnp.dot(left, kbuf[b, i, 0], preferred_element_type=jnp.float32)
                two = jnp.dot(left, kbuf[b, i, 1], preferred_element_type=jnp.float32)
                real = factor * (one[:nv] + two[nv:])
                imag = factor * (one[nv:] - two[:nv])
                gbuf[b, t, i, 0] = real.astype(jnp.bfloat16)
                gbuf[b, t, i, 1] = imag.astype(jnp.bfloat16)

    @pl.loop(1, m)
    def _(d):
        t = origin(d)
        for e in range(nf):
            b_move(t, other(e), t, other(e)).wait_recv()
        backward(t)
        for b in range(2):
            g_move(t, b, q).start()

    b_own.wait()
    for e in range(1, nf):
        b_move(q, other(e), q, other(e)).wait_recv()
    backward(q)
    for b in range(2):
        g_own[b].start()

    for i, c in pieces:
        k_move(i, c).wait_send()
    for e in range(1, nf):
        for i in range(local_f):
            p_move(q, other(e), i, q, f).wait_send()
        b_move(q, other(e), q, f).wait_send()

    @pl.loop(1, m)
    def _(d):
        t = origin(d)
        for e in range(nf):
            for i in range(local_f):
                p_move(t, other(e), i, q, f).wait_send()
            b_move(t, other(e), q, f).wait_send()
        for b in range(2):
            x_move(t, b, q).wait_send()
            g_move(t, b, q).wait_send()
            g_move(t, b, t).wait_recv()

    for b in range(2):
        g_own[b].wait()


def local(n, nf, kernel, sources, observed, gate_start, gate_length):
    local_f, _, rw, span = kernel.shape
    nv, ns = sources.shape[2:]
    half, samples = observed.shape[:2]
    count = nf * local_f
    m = n // 2
    table = jnp.asarray(transform_tables(count, samples).reshape(-1))
    gate_shape = (1, half)
    mis_shape = (samples, nv, half)
    held = 2 * sources.size + 4 * observed.size
    piece = (local_f, 2, nv, half)
    hbm_spec = pl.BlockSpec(memory_space=pltpu.HBM)
    vmem_spec = pl.BlockSpec(memory_space=pltpu.VMEM)
    dma = pltpu.SemaphoreType.DMA
    gradient, misfit = pl.pallas_call(
        functools.partial(body, n, nf, (ns / rw) ** 0.5),
        out_shape=(
            jax.ShapeDtypeStruct(sources.shape, jnp.bfloat16),
            jax.ShapeDtypeStruct(mis_shape, jnp.float32),
        ),
        in_specs=[hbm_spec, hbm_spec, hbm_spec,
                  hbm_spec, hbm_spec, hbm_spec],
        out_specs=(vmem_spec, vmem_spec),
        scratch_shapes=[
            pltpu.VMEM((2,) + kernel.shape, jnp.bfloat16),
            pltpu.VMEM((2, local_f, m, 2, nv, span), jnp.bfloat16),
            pltpu.VMEM((local_f, 2, m, 2, nv, rw), jnp.float32),
            pltpu.VMEM((m, nf) + piece, jnp.bfloat16),
            pltpu.VMEM((m, nf) + piece, jnp.bfloat16),
            pltpu.VMEM((count, 2, nv, half), jnp.float32),
            pltpu.VMEM((samples, nv, half), jnp.float32),
            pltpu.VMEM((nf,) + piece, jnp.bfloat16),
            pltpu.VMEM((local_f, m, 2, nv, nf * half), jnp.bfloat16),
            pltpu.VMEM((2, m, local_f, 2, nv, span), jnp.bfloat16),
            pltpu.SMEM((2 * count * samples,), jnp.float32),
            pltpu.VMEM((2,) + gate_shape, jnp.int32),
            dma((5,)), dma((local_f, 2, 2)), dma((local_f, 2, 2)),
            dma((m, 2)), dma((m, 2)),
            dma((m, nf, local_f)), dma((m, nf, local_f)),
            dma((m, nf)), dma((m, nf)),
            dma((m, 2)), dma((m, 2)),
        ],
        compiler_params=pltpu.CompilerParams(
            collective_id=0, has_side_effects=True, vmem_limit_bytes=67043328 - held - (1 << 20)),
    )(kernel, sources, observed.transpose(1, 2, 0), table,
      gate_start.reshape(gate_shape), gate_length.reshape(gate_shape))
    return gradient, misfit.transpose(2, 0, 1)


def solution(mesh):
    n, nf = mesh.shape["vs"], mesh.shape["freq"]
    return jax.shard_map(
        functools.partial(local, n, nf),
        mesh=mesh,
        in_specs=(
            P("freq", None, None, "vs"),
            P("freq", None, "vs", None),
            P("freq", None, "vs"),
            P("freq"),
            P("freq"),
        ),
        out_specs=(P("freq", None, "vs", None), P("freq", None, "vs")),
        check_vma=False,
    )
```
